1024 devices in a mesh: section: 16 (over y, core), expert: 64 (over z, x).
Axes of the slice: x: 4, y: 8, z: 16, core: 2. Of those that a mesh axis runs over, the one named last changes fastest.
Arguments:
- act_send: bfloat16 [8192, 3584], P(('section', 'expert')), may hold values from -6 to 6
- grad_send: bfloat16 [8192, 3584], P(('section', 'expert')), may hold values from -6 to 6
- x_back: bfloat16 [8192, 3584], P(('section', 'expert')), may hold values from -6 to 6
- routes_fwd: int32 [8192, 2], P(('section', 'expert')), may hold values from 0 to 7, all different within a row; in each aligned block of 8 rows (0 to 7, 8 to 15, ...) at most 4 rows name the same one
- gates_fwd: float32 [8192, 2], P(('section', 'expert')), may hold values from 0.3 to 1
- routes_back: int32 [8192, 2], P(('section', 'expert')), may hold values from 0 to 7, all different within a row; in each aligned block of 8 rows (0 to 7, 8 to 15, ...) at most 4 rows name the same one
- gates_back: float32 [8192, 2], P(('section', 'expert')), may hold values from 0.3 to 1
- norm_gain: float32 [16, 3584], P('section'), may hold values from 0.5 to 1.5
- w_gate: bfloat16 [16, 64, 3584, 128], P('section', 'expert'), may hold values from -0.09375 to 0.09375
- w_up: bfloat16 [16, 64, 3584, 128], P('section', 'expert'), may hold values from -0.09375 to 0.09375
- w_down: bfloat16 [16, 64, 128, 3584], P('section', 'expert'), may hold values from -0.1875 to 0.1875
- stash: bfloat16 [16, 64, 64, 4, 256], P('section', 'expert'), may hold values from -6 to 6
Outputs:
- outbound: bfloat16 [8192, 3584], P(('section', 'expert'))
- input_grad: bfloat16 [8192, 3584], P(('section', 'expert'))
The draws below stay inside these ranges and needn't reach their ends.
Inputs may be any that keep to these rules, and one draw needn't show every extreme that they name: `routes_fwd`: each row names 2 different experts; among the rows of one device no expert is named more than 4 times, a bound that some block reaches. `routes_back`: each row names 2 different experts; among the rows of one device no expert is named more than 4 times, a bound that some block reaches.
All inputs are finite; a program needn't handle non-finite values.
Results may differ from the reference program's by a relative error of at most 0.0055.
Values may be sent and summed in bfloat16 or wider, within the bound.
A program may use at most 32 MiB of HBM per device.

```python
import math
import jax
import jax.numpy as jnp
import numpy as np
from jax import lax

D = 3584
HID_DEV = 128
TOP = 2
TOK_DEV = 8
SPLIT = 8
EXP_HIDDEN = 1024
EXPERTS = 8
CAP = 4
TOKENS = 8192
N_SECTION = 16
N_EXPERT = 64


def levels(own_key, extent, pieces, least, top_value):
    factor_of = 1.0
    for axis_at, shards_of in pieces:
        steps = jax.random.uniform(jax.random.fold_in(jax.random.fold_in(own_key, 6), axis_at), (shards_of,), jnp.float32, least / len(pieces), top_value / len(pieces))
        factor_of = factor_of * jnp.repeat(jnp.exp(steps), extent[axis_at] // shards_of).reshape((-1,) + (1,) * (len(extent) - 1 - axis_at))
    return factor_of


def assign_block(own_key, own, number, rows, amount, top, most, lean):
    order = jax.random.permutation(own_key, amount)
    packed, ordinary = load_shares(amount, rows * top, most, lean, True), load_shares(amount, rows * top, most, lean, False)
    places = jnp.arange(amount)

    def named(tallies, offset_by):
        used = int((tallies > 0).sum())
        fixed = max(1, used // 4)
        shifted = fixed + (places - fixed + offset_by * (used - fixed)) % max(1, amount - fixed)
        return jnp.zeros((amount,), jnp.int32).at[order[jnp.where(places < fixed, places, shifted)]].set(jnp.asarray(tallies, jnp.int32))

    tallies = jnp.where(number % 4 == 0, named(packed, number // 4), named(ordinary, number - number // 4 - 1))
    mixed = jax.random.permutation(jax.random.fold_in(own, 3), amount)
    donor, sink = mixed[0:amount // 2 * 2:2], mixed[1:amount // 2 * 2:2]
    slack = jnp.minimum(tallies[donor] - 1, most - tallies[sink]) // 2
    slack = jnp.where((donor == order[0]) | (sink == order[0]) | (tallies[sink] == 0), 0, jnp.maximum(slack, 0))
    shifted = jax.random.randint(jax.random.fold_in(own, 4), (amount // 2,), 0, 1 << 20) % (slack + 1)
    tallies = tallies.at[donor].add(-shifted).at[sink].add(shifted)
    members = jnp.searchsorted(jnp.cumsum(tallies), jnp.arange(rows * top), side="right").astype(jnp.int32)
    table = members.reshape(top, rows).T
    table = table[jax.random.permutation(jax.random.fold_in(own, 1), rows)]
    offset_by = jax.random.randint(jax.random.fold_in(own, 2), (rows, 1), 0, top)
    return jnp.take_along_axis(table, (jnp.arange(top)[None, :] + offset_by) % top, axis=1)


def load_shares(amount, total, most, skew, full):
    portions = [(1 << 20) // math.isqrt(standing ** skew) + 1 for standing in range(1, amount + 1)]
    largest = most if full else min(most, max(-(-total // amount), total * portions[0] // sum(portions)))
    least = 1 if total - largest >= amount - 1 else 0
    holding, spare = [largest] + [least] * (amount - 1), total - largest - least * (amount - 1)
    while spare > 0:
        movable = [i for i in range(1, amount) if holding[i] < largest] or [i for i in range(1, amount) if holding[i] < most]
        mass, left = sum([portions[i] for i in movable]), spare
        for i in movable:
            extra = min(most - holding[i], max(1, left * portions[i] // mass), spare)
            holding[i] = holding[i] + extra
            spare = spare - extra
    return np.array(holding)


def noise(key, shape, deviation, bound, split=(), kind=jnp.bfloat16):
    result = deviation * jax.random.normal(key, shape, jnp.float32)
    if split:
        result = result * levels(key, shape, split, -0.22, 0.18)
    return jnp.clip(result, -bound, bound).astype(kind)


def setup_inputs(seed: int = 0) -> dict:
    splits = jax.random.split(jax.random.key(seed), 13)
    act_send = noise(splits[0], (TOKENS, D), 1.0, 6.0, ((0, 1024),))
    grad_send = noise(splits[1], (TOKENS, D), 1.0, 6.0, ((0, 1024),))
    x_back = noise(splits[2], (TOKENS, D), 1.0, 6.0, ((0, 1024),))
    routes_fwd_keys = jax.random.split(jax.random.fold_in(splits[3], 1), TOKENS // TOK_DEV)
    routes_fwd_turns = jax.random.permutation(jax.random.fold_in(splits[3], 3), TOKENS // TOK_DEV)
    routes_fwd = jax.vmap(lambda own, number: assign_block(jax.random.fold_in(splits[3], 2), own, number, TOK_DEV, EXPERTS, TOP, CAP, 2))(routes_fwd_keys, routes_fwd_turns).reshape((TOKENS, TOP))
    gates_fwd = jnp.clip(0.3 + 0.7 * jax.random.uniform(splits[4], (TOKENS, TOP), jnp.float32) ** levels(splits[4], (TOKENS, TOP), ((0, 1024),), -0.2, 0.2), 0.3, 1.0)
    routes_back_keys = jax.random.split(jax.random.fold_in(splits[5], 1), TOKENS // TOK_DEV)
    routes_back_turns = jax.random.permutation(jax.random.fold_in(splits[5], 3), TOKENS // TOK_DEV)
    routes_back = jax.vmap(lambda own, number: assign_block(jax.random.fold_in(splits[5], 2), own, number, TOK_DEV, EXPERTS, TOP, CAP, 2))(routes_back_keys, routes_back_turns).reshape((TOKENS, TOP))
    gates_back = jnp.clip(0.3 + 0.7 * jax.random.uniform(splits[6], (TOKENS, TOP), jnp.float32) ** levels(splits[6], (TOKENS, TOP), ((0, 1024),), -0.2, 0.2), 0.3, 1.0)
    norm_gain = jnp.clip(1.0 + 0.1 * jax.random.normal(splits[7], (N_SECTION, D), jnp.float32), 0.5, 1.5)
    w_gate = noise(splits[8], (N_SECTION, N_EXPERT, D, HID_DEV), D ** -0.5, 0.09375, ((0, 16), (1, 64)))
    w_up = noise(splits[9], (N_SECTION, N_EXPERT, D, HID_DEV), D ** -0.5, 0.09375, ((0, 16), (1, 64)))
    w_down = noise(splits[10], (N_SECTION, N_EXPERT, HID_DEV, D), EXP_HIDDEN ** -0.5, 0.1875, ((0, 16), (1, 64)))
    stash = noise(splits[11], (N_SECTION, N_EXPERT, N_EXPERT, CAP, 2 * HID_DEV), 1.0, 6.0, ((0, 16), (1, 64)))
    return dict(act_send=act_send, grad_send=grad_send, x_back=x_back, routes_fwd=routes_fwd, gates_fwd=gates_fwd, routes_back=routes_back, gates_back=gates_back, norm_gain=norm_gain, w_gate=w_gate, w_up=w_up, w_down=w_down, stash=stash)


EPSILON = 1e-06
HIGHEST = lax.Precision.HIGHEST

def slot_tables(routes, gates, experts, capacity):
    tokens_here = routes.shape[0]
    chosen = routes.reshape(-1)
    onehot = (chosen[:, None] == jnp.arange(experts, dtype=jnp.int32)[None, :]).astype(jnp.int32)
    earlier = jnp.cumsum(onehot, axis=0) - onehot
    within = lax.optimization_barrier(jnp.sum(earlier * onehot, axis=1))
    target = chosen * capacity + within
    slot_table = (target[:, None] == jnp.arange(experts * capacity, dtype=jnp.int32)[None, :]).astype(jnp.float32)
    slot_table = slot_table.reshape(tokens_here, routes.shape[1], experts * capacity)
    occupancy = lax.optimization_barrier(jnp.sum(slot_table, axis=1)).T
    weighted = lax.optimization_barrier(jnp.sum(slot_table * gates[:, :, None].astype(jnp.float32), axis=1))
    return (occupancy, weighted)

def normalize(values, scale_row):
    factor = lax.rsqrt(lax.optimization_barrier(jnp.mean(values * values, axis=-1, keepdims=True)) + EPSILON)
    return (values * factor * scale_row, factor)

def section_pass(inputs):
    inbound, cotangent, saved_input, routes_fwd, gates_fwd, routes_back, gates_back, scale_row, gate_all, up_all, down_all, stash_all = inputs
    normed = normalize(inbound.astype(jnp.float32), scale_row)[0].astype(jnp.bfloat16)
    tables_fwd = jax.vmap(lambda routes, gates: slot_tables(routes, gates, EXPERTS, CAP))(routes_fwd, gates_fwd)
    occupancy_fwd, weighted_fwd = tables_fwd
    slot_rows = jnp.einsum('skt,std->skd', occupancy_fwd, normed.astype(jnp.float32)).astype(jnp.bfloat16)
    slot_rows = slot_rows.reshape(N_EXPERT, EXPERTS, CAP, D)

    def device_forward(device):
        inputs_here = jnp.take(slot_rows, device // SPLIT, axis=1).reshape(-1, D)
        gate_pre = jnp.dot(inputs_here, gate_all[device], preferred_element_type=jnp.float32)
        up_pre = jnp.dot(inputs_here, up_all[device], preferred_element_type=jnp.float32)
        hidden = (jax.nn.silu(gate_pre) * up_pre).astype(jnp.bfloat16)
        return jnp.dot(hidden, down_all[device], preferred_element_type=jnp.float32).astype(jnp.bfloat16)
    partials = lax.map(device_forward, jnp.arange(N_EXPERT, dtype=jnp.int32))
    summed = partials.astype(jnp.float32).reshape(EXPERTS, SPLIT, N_EXPERT, CAP, D).sum(axis=1)
    summed = summed.transpose(1, 0, 2, 3).reshape(N_EXPERT, EXPERTS * CAP, D)
    mixture = jnp.einsum('stk,skd->std', weighted_fwd, summed, precision=HIGHEST)
    outbound = (inbound.astype(jnp.float32) + mixture).astype(jnp.bfloat16)
    tables_back = jax.vmap(lambda routes, gates: slot_tables(routes, gates, EXPERTS, CAP))(routes_back, gates_back)
    occupancy_back, weighted_back = tables_back
    grad_rows = jnp.einsum('stk,std->skd', weighted_back, cotangent.astype(jnp.float32), precision=HIGHEST).astype(jnp.bfloat16)
    grad_rows = grad_rows.reshape(N_EXPERT, EXPERTS, CAP, D)

    def device_backward(device):
        grad_here = jnp.take(grad_rows, device // SPLIT, axis=1).reshape(-1, D)
        saved_pre = stash_all[device].reshape(-1, 2 * HID_DEV).astype(jnp.float32)
        gate_pre = saved_pre[:, :HID_DEV]
        up_pre = saved_pre[:, HID_DEV:]
        grad_hidden = jnp.dot(grad_here, down_all[device].T, preferred_element_type=jnp.float32)
        sigmoid = jax.nn.sigmoid(gate_pre)
        d_gate = (grad_hidden * up_pre * sigmoid * (1.0 + gate_pre * (1.0 - sigmoid))).astype(jnp.bfloat16)
        d_up = (grad_hidden * gate_pre * sigmoid).astype(jnp.bfloat16)
        total = jnp.dot(d_gate, gate_all[device].T, preferred_element_type=jnp.float32)
        total = total + jnp.dot(d_up, up_all[device].T, preferred_element_type=jnp.float32)
        return total.astype(jnp.bfloat16)
    grad_parts = lax.map(device_backward, jnp.arange(N_EXPERT, dtype=jnp.int32))
    grad_summed = grad_parts.astype(jnp.float32).reshape(EXPERTS, SPLIT, N_EXPERT, CAP, D).sum(axis=1)
    grad_summed = grad_summed.transpose(1, 0, 2, 3).reshape(N_EXPERT, EXPERTS * CAP, D)
    grad_normed = jnp.einsum('skt,skd->std', occupancy_back, grad_summed, precision=HIGHEST)
    saved32 = saved_input.astype(jnp.float32)
    factor = normalize(saved32, scale_row)[1]
    scaled_grad = grad_normed * scale_row
    through = factor * scaled_grad - saved32 * factor ** 3 * lax.optimization_barrier(jnp.mean(scaled_grad * saved32, axis=-1, keepdims=True))
    input_grad = (cotangent.astype(jnp.float32) + through).astype(jnp.bfloat16)
    return (outbound, input_grad)

def reference(act_send, grad_send, x_back, routes_fwd, gates_fwd, routes_back, gates_back, norm_gain, w_gate, w_up, w_down, stash):

    def blocks(array):
        return array.reshape(N_SECTION, N_EXPERT, TOK_DEV, array.shape[-1])
    inbound = jnp.roll(blocks(act_send), 1, axis=0)
    cotangent = jnp.roll(blocks(grad_send), -1, axis=0)
    results = lax.map(section_pass, (inbound, cotangent, blocks(x_back), blocks(routes_fwd), blocks(gates_fwd), blocks(routes_back), blocks(gates_back), norm_gain, w_gate, w_up, w_down, stash))
    outbound, input_grad = results
    return (outbound.reshape(TOKENS, D), input_grad.reshape(TOKENS, D))
```

```python
import functools

import jax
import jax.numpy as jnp
from jax import lax
from jax.experimental import pallas as pl
from jax.experimental.pallas import tpu as pltpu
from jax.sharding import PartitionSpec as P

EPSILON = 1e-06
HIGHEST = lax.Precision.HIGHEST
MESH = pl.DeviceIdType.MESH
F32 = jnp.float32
BF16 = jnp.bfloat16

PLANES = 16
COLS = 4
STEPS = 8
EXPERTS = 8
CAP = 4


def kernel(
    act, grad, x_back, routes_fwd, gates_fwd, routes_back, gates_back, gain, w_gate, w_up, w_down, stash,
    outbound, input_grad,
    wgu, wdn, inb, cot, slots, xb, hid, ob, ra, rb, fl, fr, keep, ps, pr, ts, fb,
    shift_send, shift_recv, load_sem, send, zr, pr_in, lr, rr, fa, fbs, ra_in, rb_in, fl_in, fr_in, pb_in, fin,
):
    width = act.shape[1]
    half = width // 2
    quarter = half // 2
    n_section = lax.axis_size("section")
    s = lax.axis_index("section")
    me = lax.axis_index("expert")
    z = me // COLS
    x = lax.rem(me, COLS)
    parity = lax.rem(z, 2)
    sg = 2 * parity - 1
    mine = z // 2

    def plane(v):
        return lax.rem(v + 2 * PLANES, PLANES)

    def at_plane(v):
        return {"expert": plane(v) * COLS + x}

    right = {"expert": z * COLS + lax.rem(x + 1, COLS)}
    left = {"expert": z * COLS + lax.rem(x + COLS - 1, COLS)}
    partner = at_plane(z - sg)
    after = {"section": lax.rem(s + 1, n_section)}
    before = {"section": lax.rem(s + n_section - 1, n_section)}

    def remote(src, dst, send_sem, recv_sem, device):
        pltpu.make_async_remote_copy(
            src_ref=src, dst_ref=dst, send_sem=send_sem, recv_sem=recv_sem, device_id=device, device_id_type=MESH
        ).start()

    def arrive(ref, sem):
        pltpu.make_async_copy(ref, ref, sem).wait()

    loads = [
        pltpu.make_async_copy(w_gate, wgu.at[:, 0:128], load_sem.at[0]),
        pltpu.make_async_copy(w_up, wgu.at[:, 128:256], load_sem.at[1]),
        pltpu.make_async_copy(w_down, wdn, load_sem.at[2]),
    ]
    for load in loads:
        load.start()

    barrier = pltpu.get_barrier_semaphore()
    everyone = [after, before, left, right, partner]
    everyone += [at_plane(z + sg * d) for d in range(1, STEPS)]
    everyone += [at_plane(z - sg * 2 * k) for k in range(1, STEPS // 2)]
    for device in everyone:
        pl.semaphore_signal(barrier, inc=1, device_id=device, device_id_type=MESH)
    pl.semaphore_wait(barrier, len(everyone))

    remote(act, inb, shift_send.at[0], shift_recv.at[0], after)
    remote(grad, cot, shift_send.at[1], shift_recv.at[1], before)

    def tables(routes_ref, gates_ref):
        lane = lax.broadcasted_iota(jnp.int32, (8, 64), 1)
        expert = lane >> 3
        rank = (lane & 3).astype(F32)
        m0 = jnp.where(routes_ref[:, 0:1] == expert, 1.0, 0.0)
        m1 = jnp.where(routes_ref[:, 1:2] == expert, 1.0, 0.0)
        m = m0 + m1
        lower = jnp.where(
            lax.broadcasted_iota(jnp.int32, (8, 8), 0) > lax.broadcasted_iota(jnp.int32, (8, 8), 1), 1.0, 0.0
        )
        earlier = jnp.dot(lower, m, preferred_element_type=F32, precision=HIGHEST)
        here = jnp.where(earlier == rank, m, 0.0)
        weighted = jnp.where(here > 0.0, m0 * gates_ref[:, 0:1] + m1 * gates_ref[:, 1:2], 0.0)
        return here, weighted

    here_f, weight_f = tables(routes_fwd, gates_fwd)
    here_b, weight_b = tables(routes_back, gates_back)
    top_lane = (lax.broadcasted_iota(jnp.int32, (8, 64), 1) & 4) == 0

    def row_top(rows):
        return (lax.broadcasted_iota(jnp.int32, (rows, 1), 0) & 4) == 0

    def pick(table, values, precision):
        dims = (((0,), (0,)), ((), ()))
        a = lax.dot_general(table, values[:, :half], dims, preferred_element_type=F32, precision=precision)
        b = lax.dot_general(table, values[:, half:], dims, preferred_element_type=F32, precision=precision)
        return jnp.where(row_top(64), a, b).astype(BF16).reshape(EXPERTS, 8, half)

    def send_slots(f):
        for k in range(STEPS // 2):
            same = plane(z - sg * 2 * k)
            if k == 0:
                pltpu.make_async_copy(slots.at[f, mine], xb.at[f, 0, 0, 0], zr.at[f, 0]).start()
            else:
                remote(slots.at[f, same // 2], xb.at[f, 0, 2 * k, 0], send.at[f, 0], zr.at[f, 2 * k], at_plane(same))
            other = plane(z + sg * (2 * k + 1))
            remote(
                slots.at[f, other // 2], xb.at[f, 0, 2 * k + 1, 0], send.at[f, 0], zr.at[f, 2 * k + 1], at_plane(other)
            )

    arrive(inb, shift_recv.at[0])
    inbound = inb[...].astype(F32)
    factor = lax.rsqrt(jnp.mean(inbound * inbound, axis=-1, keepdims=True) + EPSILON)
    normed = (inbound * factor * gain[...]).astype(BF16)
    slots[0] = pick(here_f.astype(BF16), normed, None)
    send_slots(0)
    arrive(cot, shift_recv.at[1])
    slots[1] = pick(weight_b, cot[...].astype(F32), HIGHEST)
    send_slots(1)

    def to_partner(f, d):
        arrive(xb.at[f, 0, d, 0], zr.at[f, d])
        remote(xb.at[f, 0, d, 0], xb.at[f, 0, d, 1], send.at[f, 1], pr_in.at[f, d], partner)

    def to_sides(f, d):
        arrive(xb.at[f, 0, d, 1], pr_in.at[f, d])
        remote(xb.at[f, 0, d], xb.at[f, 1, d], send.at[f, 2], lr.at[f, d], right)
        remote(xb.at[f, 0, d], xb.at[f, 2, d], send.at[f, 3], rr.at[f, d], left)

    def to_far(f, d):
        arrive(xb.at[f, 1, d], lr.at[f, d])
        remote(
            xb.at[f, 1, d, :, :, 0:quarter], xb.at[f, 3, d, :, :, 0:quarter], send.at[f, 4], fa.at[f, d], right
        )
        arrive(xb.at[f, 2, d], rr.at[f, d])
        remote(
            xb.at[f, 2, d, :, :, quarter:half], xb.at[f, 3, d, :, :, quarter:half], send.at[f, 5], fbs.at[f, d], left
        )

    def dispatch_step(f, j):
        @pl.when(j < STEPS)
        def _():
            to_partner(f, j)

        @pl.when(jnp.logical_and(j >= 1, j < STEPS + 1))
        def _():
            to_sides(f, j - 1)

        @pl.when(j >= 3)
        def _():
            to_far(f, j - 3)

    def far_arrived(f):
        @pl.loop(0, STEPS)
        def _(d):
            arrive(xb.at[f, 3, d, :, :, 0:quarter], fa.at[f, d])
            arrive(xb.at[f, 3, d, :, :, quarter:half], fbs.at[f, d])

    ROWS = STEPS * 2 * 8
    top = row_top(ROWS)

    def both_halves(a, b):
        v = jnp.where(top, a, b)
        return v + jnp.where(top, pltpu.roll(v, ROWS - 4, 0), pltpu.roll(v, 4, 0))

    def rows_of(f, rel):
        return xb[f, rel].astype(F32).reshape(ROWS, half).astype(BF16)

    def forward_hidden(rel):
        rows = rows_of(0, rel)
        a = jnp.dot(rows, wgu[0:half, :], preferred_element_type=F32)
        b = jnp.dot(rows, wgu[half:width, :], preferred_element_type=F32)
        v = both_halves(a, b)
        gate, up = v[:, :128], v[:, 128:]
        hid[rel] = (gate / (1.0 + jnp.exp(-gate)) * up).astype(BF16)

    def forward_out(rel):
        h = hid[rel]
        a = jnp.dot(h, wdn[:, 0:half], preferred_element_type=F32)
        b = jnp.dot(h, wdn[:, half:width], preferred_element_type=F32)
        ob[0, rel] = jnp.where(top, a, b).reshape(STEPS, 2, 8, half).astype(BF16)

    NT = (((1,), (1,)), ((), ()))

    def backward(rel):
        rows = rows_of(1, rel)
        a = lax.dot_general(rows, wdn[:, 0:half], NT, preferred_element_type=F32)
        b = lax.dot_general(rows, wdn[:, half:width], NT, preferred_element_type=F32)
        dh = both_halves(a, b)
        col = lax.rem(x + jnp.where(rel == 1, 3, jnp.where(rel == 2, 1, jnp.where(rel == 3, 2, 0))), COLS)
        saved = []
        for d in range(STEPS):
            for zs in (plane(z + sg * d), plane(z - sg * (1 + d))):
                saved.append(stash[zs * COLS + col].astype(F32))
        saved = jnp.concatenate(saved, axis=0)
        gate, up = saved[:, :128], saved[:, 128:]
        sig = 1.0 / (1.0 + jnp.exp(-gate))
        d_gate = dh * up * sig * (1.0 + gate * (1.0 - sig))
        d_up = dh * gate * sig
        d_both = jnp.concatenate([d_gate, d_up], axis=1).astype(BF16)
        a = lax.dot_general(d_both, wgu[0:half, :], NT, preferred_element_type=F32)
        b = lax.dot_general(d_both, wgu[half:width, :], NT, preferred_element_type=F32)
        ob[1, rel] = jnp.where(top, a, b).reshape(STEPS, 2, 8, half).astype(BF16)

    def far_out(f):
        @pl.loop(0, STEPS)
        def _(j):
            d = STEPS - 1 - j
            remote(ob.at[f, 3, d, :, :, 0:quarter], ra.at[f, d], send.at[f, 6], ra_in.at[f, d], left)
            remote(ob.at[f, 3, d, :, :, quarter:half], rb.at[f, d], send.at[f, 7], rb_in.at[f, d], right)

    def sides_out(f, d):
        arrive(ra.at[f, d], ra_in.at[f, d])
        v = ob[f, 1, d, :, :, 0:quarter].astype(F32) + ra[f, d].astype(F32)
        ob[f, 1, d, :, :, 0:quarter] = v.astype(BF16)
        remote(ob.at[f, 1, d], fr.at[f, d], send.at[f, 8], fr_in.at[f, d], left)
        arrive(rb.at[f, d], rb_in.at[f, d])
        v = ob[f, 2, d, :, :, quarter:half].astype(F32) + rb[f, d].astype(F32)
        ob[f, 2, d, :, :, quarter:half] = v.astype(BF16)
        remote(ob.at[f, 2, d], fl.at[f, d], send.at[f, 9], fl_in.at[f, d], right)

    def pair_out(f, d):
        arrive(fr.at[f, d], fr_in.at[f, d])
        arrive(fl.at[f, d], fl_in.at[f, d])
        v = ob[f, 0, d].astype(F32) + fr[f, d].astype(F32) + fl[f, d].astype(F32)
        keep[f, d] = v[0]
        ps[f, d] = v[1].astype(BF16)
        remote(ps.at[f, d], pr.at[f, d], send.at[f, 10], pb_in.at[f, d], partner)

    def source_out(f, d):
        arrive(pr.at[f, d], pb_in.at[f, d])
        ts[f, d] = (keep[f, d] + pr[f, d].astype(F32)).astype(BF16)

        @pl.when(d == 0)
        def _():
            pltpu.make_async_copy(ts.at[f, d], fb.at[f, mine], fin.at[f, mine]).start()

        @pl.when(d > 0)
        def _():
            remote(ts.at[f, d], fb.at[f, mine], send.at[f, 11], fin.at[f, mine], at_plane(z + sg * d))

    def gathered(f, table):
        for e in range(EXPERTS):
            arrive(fb.at[f, e], fin.at[f, e])
        rows = fb[f].astype(F32).reshape(EXPERTS * 8, half)
        a = jnp.dot(jnp.where(top_lane, table, 0.0), rows, preferred_element_type=F32, precision=HIGHEST)
        b = jnp.dot(jnp.where(top_lane, 0.0, table), rows, preferred_element_type=F32, precision=HIGHEST)
        return jnp.concatenate([a, b], axis=1)

    @pl.loop(0, STEPS + 3)
    def _(j):
        dispatch_step(0, j)

    for load in loads:
        load.wait()

    @pl.loop(0, STEPS + 3)
    def _(j):
        dispatch_step(1, j)

        @pl.when(jnp.logical_and(lax.rem(j, 2) == 0, jnp.logical_and(j >= 2, j < 10)))
        def _():
            rel = (j - 2) // 2

            @pl.when(rel == 3)
            def _():
                far_arrived(0)

            forward_hidden(rel)

    @pl.loop(0, COLS)
    def _(j):
        rel = COLS - 1 - j
        forward_out(rel)

        @pl.when(j == 0)
        def _():
            far_out(0)

    far_arrived(1)

    @pl.loop(0, COLS)
    def _(j):
        rel = COLS - 1 - j
        backward(rel)

        @pl.when(j == 0)
        def _():
            far_out(1)

        sides_out(0, STEPS - 1 - 2 * j)
        sides_out(0, STEPS - 2 - 2 * j)

    @pl.loop(0, STEPS + 1)
    def _(j):
        @pl.when(j < STEPS)
        def _():
            sides_out(1, STEPS - 1 - j)
            pair_out(0, STEPS - 1 - j)

        @pl.when(j >= 1)
        def _():
            source_out(0, STEPS - j)

    @pl.loop(0, STEPS + 1)
    def _(j):
        @pl.when(j < STEPS)
        def _():
            pair_out(1, STEPS - 1 - j)

        @pl.when(j >= 1)
        def _():
            source_out(1, STEPS - j)

    outbound[...] = (inb[...].astype(F32) + gathered(0, weight_f)).astype(BF16)

    grad_normed = gathered(1, here_b)
    saved = x_back[...].astype(F32)
    factor_b = lax.rsqrt(jnp.mean(saved * saved, axis=-1, keepdims=True) + EPSILON)
    scaled = grad_normed * gain[...]
    through = factor_b * scaled - saved * (factor_b * factor_b * factor_b) * jnp.mean(
        scaled * saved, axis=-1, keepdims=True
    )
    input_grad[...] = (cot[...].astype(F32) + through).astype(BF16)

    arrive(act, shift_send.at[0])
    arrive(grad, shift_send.at[1])
    for f in range(2):
        arrive(xb.at[f, 0, 1:8, 0], send.at[f, 0])
        arrive(xb.at[f, 0, :, 0], send.at[f, 1])
        arrive(xb.at[f, 0], send.at[f, 2])
        arrive(xb.at[f, 0], send.at[f, 3])
        arrive(xb.at[f, 1, :, :, :, 0:quarter], send.at[f, 4])
        arrive(xb.at[f, 2, :, :, :, quarter:half], send.at[f, 5])
        arrive(ra.at[f], send.at[f, 6])
        arrive(rb.at[f], send.at[f, 7])
        arrive(ob.at[f, 1], send.at[f, 8])
        arrive(ob.at[f, 2], send.at[f, 9])
        arrive(ps.at[f], send.at[f, 10])
        arrive(ts.at[f, 1:8], send.at[f, 11])


def body(
    act_send, grad_send, x_back, routes_fwd, gates_fwd, routes_back, gates_back, norm_gain, w_gate, w_up, w_down, stash
):
    rows, width = act_send.shape
    half = width // 2
    any_space = pl.BlockSpec(memory_space=pl.ANY)
    vmem = pl.BlockSpec(memory_space=pltpu.VMEM)
    twice = jnp.concatenate([stash[0, 0], stash[0, 0]], axis=1)
    dma = pltpu.SemaphoreType.DMA
    return pl.pallas_call(
        kernel,
        out_shape=(
            jax.ShapeDtypeStruct((rows, width), BF16),
            jax.ShapeDtypeStruct((rows, width), BF16),
        ),
        in_specs=[any_space, any_space] + [vmem] * 6 + [any_space] * 3 + [vmem],
        out_specs=(vmem, vmem),
        scratch_shapes=[
            pltpu.VMEM((width, 256), BF16),
            pltpu.VMEM((128, width), BF16),
            pltpu.VMEM((rows, width), BF16),
            pltpu.VMEM((rows, width), BF16),
            pltpu.VMEM((2, EXPERTS, 8, half), BF16),
            pltpu.VMEM((2, COLS, STEPS, 2, 8, half), BF16),
            pltpu.VMEM((COLS, STEPS * 16, 128), BF16),
            pltpu.VMEM((2, COLS, STEPS, 2, 8, half), BF16),
            pltpu.VMEM((2, STEPS, 2, 8, half // 2), BF16),
            pltpu.VMEM((2, STEPS, 2, 8, half // 2), BF16),
            pltpu.VMEM((2, STEPS, 2, 8, half), BF16),
            pltpu.VMEM((2, STEPS, 2, 8, half), BF16),
            pltpu.VMEM((2, STEPS, 8, half), F32),
            pltpu.VMEM((2, STEPS, 8, half), BF16),
            pltpu.VMEM((2, STEPS, 8, half), BF16),
            pltpu.VMEM((2, STEPS, 8, half), BF16),
            pltpu.VMEM((2, EXPERTS, 8, half), BF16),
            dma((2,)),
            dma((2,)),
            dma((3,)),
            dma((2, 12)),
        ]
        + [dma((2, STEPS))] * 12,
        compiler_params=pltpu.CompilerParams(
            collective_id=0, has_side_effects=True, vmem_limit_bytes=48 * 1024 * 1024
        ),
    )(
        act_send, grad_send, x_back, routes_fwd, gates_fwd, routes_back, gates_back, norm_gain,
        w_gate[0, 0], w_up[0, 0], w_down[0, 0], twice,
    )


def solution(mesh):
    rows = P(("section", "expert"), None)
    held = P("section", "expert", None, None)
    return jax.shard_map(
        body,
        mesh=mesh,
        in_specs=(rows,) * 7 + (P("section", None), held, held, held, P("section", "expert", None, None, None)),
        out_specs=(rows, rows),
        check_vma=False,
    )
```

```python
import functools

import jax
import jax.numpy as jnp
from jax import lax
from jax.experimental import pallas as pl
from jax.experimental.pallas import tpu as pltpu
from jax.sharding import PartitionSpec as P

EPSILON = 1e-06
HIGHEST = lax.Precision.HIGHEST
MESH = pl.DeviceIdType.MESH
F32 = jnp.float32
BF16 = jnp.bfloat16

PLANES = 16
COLS = 4
STEPS = 8
EXPERTS = 8
CAP = 4
AHEAD = 6
LAGS = (0, 1, 3, 6, 8, 11, 13)


def kernel(
    act, grad, x_back_in, routes_fwd_in, gates_fwd_in, routes_back_in, gates_back_in, gain_in, w_gate, w_up, w_down,
    stash_in,
    outbound, input_grad,
    x_back, routes_fwd, gates_fwd, routes_back, gates_back, gain, stash, wgu, wdn, inb, cot, slots, xb, ob, ra, rb, fl, fr, keep, ps, pr, ts, fb,
    shift_send, shift_recv, load_sem, send, zr, pr_in, lr, rr, fa, fbs, ra_in, rb_in, fl_in, fr_in, pb_in, fin,
):
    width = act.shape[1]
    half = width // 2
    quarter = half // 2
    n_section = lax.axis_size("section")
    s = lax.axis_index("section")
    me = lax.axis_index("expert")
    z = me // COLS
    x = lax.rem(me, COLS)
    parity = lax.rem(z, 2)
    sg = 2 * parity - 1
    mine = z // 2

    def plane(v):
        return lax.rem(v + 2 * PLANES, PLANES)

    def at_plane(v):
        return {"expert": plane(v) * COLS + x}

    right = {"expert": z * COLS + lax.rem(x + 1, COLS)}
    left = {"expert": z * COLS + lax.rem(x + COLS - 1, COLS)}
    partner = at_plane(z - sg)
    after = {"section": lax.rem(s + 1, n_section)}
    before = {"section": lax.rem(s + n_section - 1, n_section)}

    def remote(src, dst, send_sem, recv_sem, device):
        pltpu.make_async_remote_copy(
            src_ref=src, dst_ref=dst, send_sem=send_sem, recv_sem=recv_sem, device_id=device, device_id_type=MESH
        ).start()

    def arrive(ref, sem):
        pltpu.make_async_copy(ref, ref, sem).wait()

    pairs = [
        (routes_fwd_in, routes_fwd), (gates_fwd_in, gates_fwd), (routes_back_in, routes_back),
        (gates_back_in, gates_back), (gain_in, gain), (x_back_in, x_back), (stash_in, stash),
        (w_gate, wgu.at[:, 0:128]), (w_up, wgu.at[:, 128:256]), (w_down, wdn),
    ]
    loads = [pltpu.make_async_copy(src, dst, load_sem.at[i]) for i, (src, dst) in enumerate(pairs)]
    early, late = loads[:5], loads[5:]
    for load in early:
        load.start()

    barrier = pltpu.get_barrier_semaphore()
    everyone = [after, before, left, right, partner]
    everyone += [at_plane(z + sg * d) for d in range(1, STEPS)]
    everyone += [at_plane(z - sg * 2 * k) for k in range(1, STEPS // 2)]
    for device in everyone:
        pl.semaphore_signal(barrier, inc=1, device_id=device, device_id_type=MESH)
    pl.semaphore_wait(barrier, len(everyone))

    remote(act, inb, shift_send.at[0], shift_recv.at[0], after)
    remote(grad, cot, shift_send.at[1], shift_recv.at[1], before)
    for load in late:
        load.start()
    for load in early:
        load.wait()

    def tables(routes_ref, gates_ref):
        row = lax.broadcasted_iota(jnp.int32, (64, 8), 0)
        expert = row >> 3
        rank = (row & 3).astype(F32)
        m0 = jnp.where(routes_ref[0:1, :] == expert, 1.0, 0.0)
        m1 = jnp.where(routes_ref[1:2, :] == expert, 1.0, 0.0)
        m = m0 + m1
        before_it = jnp.where(
            lax.broadcasted_iota(jnp.int32, (8, 8), 0) < lax.broadcasted_iota(jnp.int32, (8, 8), 1), 1.0, 0.0
        )
        earlier = jnp.dot(m.astype(BF16), before_it.astype(BF16), preferred_element_type=F32)
        here = jnp.where(earlier == rank, m, 0.0)
        weighted = jnp.where(here > 0.0, m0 * gates_ref[0:1, :] + m1 * gates_ref[1:2, :], 0.0)
        return here, weighted

    here_f, weight_f = tables(routes_fwd, gates_fwd)
    here_b, weight_b = tables(routes_back, gates_back)

    def row_top(rows):
        return (lax.broadcasted_iota(jnp.int32, (rows, 1), 0) & 4) == 0

    def pick(table, values):
        chosen = table.astype(BF16)
        a = jnp.dot(chosen, values[:, :half], preferred_element_type=F32)
        b = jnp.dot(chosen, values[:, half:], preferred_element_type=F32)
        return jnp.where(row_top(64), a, b)

    def put_slots(f, rows):
        slots[f] = rows.astype(BF16).reshape(EXPERTS, 8, half)

    def send_own(f):
        remote(slots.at[f, mine], xb.at[f, 0, 0, 1], send.at[f, 1], pr_in.at[f, 0], partner)
        pltpu.make_async_copy(slots.at[f, mine], xb.at[f, 0, 0, 0], zr.at[f, 0]).start()

    def send_slots(f, d):
        there = plane(z + sg * (2 * lax.rem(d, 2) - 1) * d)
        remote(slots.at[f, there // 2], xb.at[f, 0, d, 0], send.at[f, 0], zr.at[f, d], at_plane(there))

    def prepare(f):
        if f == 0:
            arrive(inb, shift_recv.at[0])
            inbound = inb[...].astype(F32)
            factor = lax.rsqrt(jnp.mean(inbound * inbound, axis=-1, keepdims=True) + EPSILON)
            put_slots(0, pick(here_f, (inbound * factor * gain[...]).astype(BF16)))
        else:
            arrive(cot, shift_recv.at[1])
            put_slots(1, pick(here_b, cot[...]) * jnp.sum(weight_b, axis=1, keepdims=True))

    def either(f, work):
        @pl.when(f == 0)
        def _():
            work(0)

        @pl.when(f == 1)
        def _():
            work(1)

    first = lax.rem(s + 1, 2)
    second = 1 - first
    either(first, prepare)
    send_own(first)
    either(second, prepare)
    send_own(second)

    def to_partner(f, d):
        arrive(xb.at[f, 0, d, 0], zr.at[f, d])

        @pl.when(d > 0)
        def _():
            remote(xb.at[f, 0, d, 0], xb.at[f, 0, d, 1], send.at[f, 1], pr_in.at[f, d], partner)

    def to_sides(f, d):
        arrive(xb.at[f, 0, d, 1], pr_in.at[f, d])
        remote(xb.at[f, 0, d], xb.at[f, 1, d], send.at[f, 2], lr.at[f, d], right)
        remote(xb.at[f, 0, d], xb.at[f, 2, d], send.at[f, 3], rr.at[f, d], left)

    def to_far(f, d):
        arrive(xb.at[f, 1, d], lr.at[f, d])
        remote(
            xb.at[f, 1, d, :, :, 0:quarter], xb.at[f, 3, d, :, :, 0:quarter], send.at[f, 4], fa.at[f, d], right
        )
        arrive(xb.at[f, 2, d], rr.at[f, d])
        remote(
            xb.at[f, 2, d, :, :, quarter:half], xb.at[f, 3, d, :, :, quarter:half], send.at[f, 5], fbs.at[f, d], left
        )

    ROWS = COLS * 2 * 8
    top = row_top(ROWS)

    def both_halves(a, b):
        v = jnp.where(top, a, b)
        return v + jnp.where(top, pltpu.roll(v, ROWS - 4, 0), pltpu.roll(v, 4, 0))

    def rows_of(f, d):
        return xb[f, :, d].astype(F32).reshape(ROWS, half).astype(BF16)

    def forward(d):
        rows = rows_of(0, d)
        a = jnp.dot(rows, wgu[0:half, :], preferred_element_type=F32)
        b = jnp.dot(rows, wgu[half:width, :], preferred_element_type=F32)
        v = both_halves(a, b)
        gate, up = v[:, :128], v[:, 128:]
        h = (gate / (1.0 + jnp.exp(-gate)) * up).astype(BF16)
        a = jnp.dot(h, wdn[:, 0:half], preferred_element_type=F32)
        b = jnp.dot(h, wdn[:, half:width], preferred_element_type=F32)
        ob[0, :, d] = jnp.where(top, a, b).reshape(COLS, 2, 8, half).astype(BF16)

    NT = (((1,), (1,)), ((), ()))

    def backward(d):
        rows = rows_of(1, d)
        a = lax.dot_general(rows, wdn[:, 0:half], NT, preferred_element_type=F32)
        b = lax.dot_general(rows, wdn[:, half:width], NT, preferred_element_type=F32)
        dh = both_halves(a, b)
        saved = []
        for step in (0, 3, 1, 2):
            col = lax.rem(x + step, COLS)
            for zs in (plane(z + sg * d), plane(z - sg * (1 + d))):
                own = stash[zs * COLS + col].astype(F32)
                saved += [own, own]
        saved = jnp.concatenate(saved, axis=0)
        gate, up = saved[:, :128], saved[:, 128:]
        sig = 1.0 / (1.0 + jnp.exp(-gate))
        d_gate = dh * up * sig * (1.0 + gate * (1.0 - sig))
        d_up = dh * gate * sig
        d_both = jnp.concatenate([d_gate, d_up], axis=1).astype(BF16)
        a = lax.dot_general(d_both, wgu[0:half, :], NT, preferred_element_type=F32)
        b = lax.dot_general(d_both, wgu[half:width, :], NT, preferred_element_type=F32)
        ob[1, :, d] = jnp.where(top, a, b).reshape(COLS, 2, 8, half).astype(BF16)

    def far_out(f, d):
        remote(ob.at[f, 3, d, :, :, 0:quarter], ra.at[f, d], send.at[f, 6], ra_in.at[f, d], left)
        remote(ob.at[f, 3, d, :, :, quarter:half], rb.at[f, d], send.at[f, 7], rb_in.at[f, d], right)

    def sides_out(f, d):
        arrive(ra.at[f, d], ra_in.at[f, d])
        v = ob[f, 1, d, :, :, 0:quarter].astype(F32) + ra[f, d].astype(F32)
        ob[f, 1, d, :, :, 0:quarter] = v.astype(BF16)
        remote(ob.at[f, 1, d], fr.at[f, d], send.at[f, 8], fr_in.at[f, d], left)
        arrive(rb.at[f, d], rb_in.at[f, d])
        v = ob[f, 2, d, :, :, quarter:half].astype(F32) + rb[f, d].astype(F32)
        ob[f, 2, d, :, :, quarter:half] = v.astype(BF16)
        remote(ob.at[f, 2, d], fl.at[f, d], send.at[f, 9], fl_in.at[f, d], right)

    def pair_out(f, d):
        arrive(fr.at[f, d], fr_in.at[f, d])
        arrive(fl.at[f, d], fl_in.at[f, d])
        v = ob[f, 0, d].astype(F32) + fr[f, d].astype(F32) + fl[f, d].astype(F32)
        keep[f, d] = v[0]
        ps[f, d] = v[1].astype(BF16)
        remote(ps.at[f, d], pr.at[f, d], send.at[f, 10], pb_in.at[f, d], partner)

    def source_out(f, d):
        arrive(pr.at[f, d], pb_in.at[f, d])
        ts[f, d] = (keep[f, d] + pr[f, d].astype(F32)).astype(BF16)

        @pl.when(d == 0)
        def _():
            pltpu.make_async_copy(ts.at[f, d], fb.at[f, mine], fin.at[f, mine]).start()

        @pl.when(d > 0)
        def _():
            remote(ts.at[f, d], fb.at[f, mine], send.at[f, 11], fin.at[f, mine], at_plane(z + sg * d))

    def gathered(f, parts):
        for e in range(EXPERTS):
            arrive(fb.at[f, e], fin.at[f, e])
        rows = fb[f].astype(F32).reshape(EXPERTS * 8, half).astype(BF16)
        dims = (((0,), (0,)), ((), ()))
        both = []
        for kept in (row_top(64), jnp.logical_not(row_top(64))):
            terms = [
                lax.dot_general(jnp.where(kept, t, 0.0).astype(BF16), rows, dims, preferred_element_type=F32)
                for t in parts
            ]
            both.append(functools.reduce(jnp.add, terms))
        return jnp.concatenate(both, axis=1)

    def compute(f, d):
        arrive(xb.at[f, 3, d, :, :, 0:quarter], fa.at[f, d])
        arrive(xb.at[f, 3, d, :, :, quarter:half], fbs.at[f, d])
        either(f, lambda which: (forward, backward)[which](d))
        far_out(f, d)

    def unit(v, work):
        work(lax.rem(first + v, 2), lax.rem(STEPS - v // 2, STEPS))

    @pl.loop(2, AHEAD)
    def _(v):
        unit(v, send_slots)

    for load in late:
        load.wait()

    stages = (to_partner, to_sides, to_far, compute, sides_out, pair_out, source_out)

    @pl.loop(0, 2 * STEPS + max(LAGS))
    def _(u):
        @pl.when(u + AHEAD < 2 * STEPS)
        def _():
            unit(u + AHEAD, send_slots)

        for lag, stage in zip(LAGS, stages):
            @pl.when(jnp.logical_and(u >= lag, u < 2 * STEPS + lag))
            def _(lag=lag, stage=stage):
                unit(u - lag, stage)

    high = weight_f.astype(BF16).astype(F32)
    middle = (weight_f - high).astype(BF16).astype(F32)
    weight_parts = [high, middle, weight_f - high - middle]
    outbound[...] = (inb[...].astype(F32) + gathered(0, weight_parts)).astype(BF16)

    grad_normed = gathered(1, [here_b])
    saved = x_back[...].astype(F32)
    factor_b = lax.rsqrt(jnp.mean(saved * saved, axis=-1, keepdims=True) + EPSILON)
    scaled = grad_normed * gain[...]
    through = factor_b * scaled - saved * (factor_b * factor_b * factor_b) * jnp.mean(
        scaled * saved, axis=-1, keepdims=True
    )
    input_grad[...] = (cot[...].astype(F32) + through).astype(BF16)

    arrive(act, shift_send.at[0])
    arrive(grad, shift_send.at[1])
    for f in range(2):
        arrive(xb.at[f, 0, 1:8, 0], send.at[f, 0])
        arrive(xb.at[f, 0, :, 0], send.at[f, 1])
        arrive(xb.at[f, 0], send.at[f, 2])
        arrive(xb.at[f, 0], send.at[f, 3])
        arrive(xb.at[f, 1, :, :, :, 0:quarter], send.at[f, 4])
        arrive(xb.at[f, 2, :, :, :, quarter:half], send.at[f, 5])
        arrive(ra.at[f], send.at[f, 6])
        arrive(rb.at[f], send.at[f, 7])
        arrive(ob.at[f, 1], send.at[f, 8])
        arrive(ob.at[f, 2], send.at[f, 9])
        arrive(ps.at[f], send.at[f, 10])
        arrive(ts.at[f, 1:8], send.at[f, 11])


def body(
    act_send, grad_send, x_back, routes_fwd, gates_fwd, routes_back, gates_back, norm_gain, w_gate, w_up, w_down, stash
):
    rows, width = act_send.shape
    half = width // 2
    hbm = pl.BlockSpec(memory_space=pltpu.HBM)
    vmem = pl.BlockSpec(memory_space=pltpu.VMEM)
    dma = pltpu.SemaphoreType.DMA
    return pl.pallas_call(
        kernel,
        out_shape=(
            jax.ShapeDtypeStruct((rows, width), BF16),
            jax.ShapeDtypeStruct((rows, width), BF16),
        ),
        in_specs=[hbm] * 12,
        out_specs=(vmem, vmem),
        scratch_shapes=[
            pltpu.VMEM((rows, width), BF16),
            pltpu.VMEM((2, rows), jnp.int32),
            pltpu.VMEM((2, rows), F32),
            pltpu.VMEM((2, rows), jnp.int32),
            pltpu.VMEM((2, rows), F32),
            pltpu.VMEM((1, width), F32),
            pltpu.VMEM(stash.shape[2:], BF16),
            pltpu.VMEM((width, 256), BF16),
            pltpu.VMEM((128, width), BF16),
            pltpu.VMEM((rows, width), BF16),
            pltpu.VMEM((rows, width), BF16),
            pltpu.VMEM((2, EXPERTS, 8, half), BF16),
            pltpu.VMEM((2, COLS, STEPS, 2, 8, half), BF16),
            pltpu.VMEM((2, COLS, STEPS, 2, 8, half), BF16),
            pltpu.VMEM((2, STEPS, 2, 8, half // 2), BF16),
            pltpu.VMEM((2, STEPS, 2, 8, half // 2), BF16),
            pltpu.VMEM((2, STEPS, 2, 8, half), BF16),
            pltpu.VMEM((2, STEPS, 2, 8, half), BF16),
            pltpu.VMEM((2, STEPS, 8, half), F32),
            pltpu.VMEM((2, STEPS, 8, half), BF16),
            pltpu.VMEM((2, STEPS, 8, half), BF16),
            pltpu.VMEM((2, STEPS, 8, half), BF16),
            pltpu.VMEM((2, EXPERTS, 8, half), BF16),
            dma((2,)),
            dma((2,)),
            dma((10,)),
            dma((2, 12)),
        ]
        + [dma((2, STEPS))] * 12,
        compiler_params=pltpu.CompilerParams(
            collective_id=0, has_side_effects=True, vmem_limit_bytes=67043328
        ),
    )(
        act_send, grad_send, x_back, routes_fwd.T, gates_fwd.T, routes_back.T, gates_back.T, norm_gain,
        w_gate[0, 0], w_up[0, 0], w_down[0, 0], stash[0, 0],
    )


def solution(mesh):
    rows = P(("section", "expert"), None)
    held = P("section", "expert", None, None)
    return jax.shard_map(
        body,
        mesh=mesh,
        in_specs=(rows,) * 7 + (P("section", None), held, held, held, P("section", "expert", None, None, None)),
        out_specs=(rows, rows),
        check_vma=False,
    )
```
